512 devices in a mesh: layer: 32 (over z, core), row: 16 (over y, x).
Axes of the slice: x: 4, y: 4, z: 16, core: 2. Of those that a mesh axis runs over, the one named last changes fastest.
Arguments:
- propagator: float32 [32, 16384, 6, 128], P('layer', 'row'), may hold values from -0.15625 to 0.15625
- col_blocks: int32 [32, 128, 6], P('layer', 'row'), may hold values from 0 to 127, as said below
- sources: bfloat16 [8, 32, 56, 16384], P(None, 'layer', None, 'row'), may hold values from -6 to 6
- incoming: bfloat16 [32, 56, 16384], P('layer', None, 'row'), may hold values from -6 to 6
Outputs:
- outgoing: bfloat16 [8, 32, 56, 16384], P(None, 'layer', None, 'row')
The draws below stay inside these ranges and needn't reach their ends.
Inputs may be any that keep to these rules, and one draw needn't show every extreme that they name: col_blocks[l, r, k] differs from r by at most 8; slot 0 is r itself, slots 1 and 2 are r - 8 and r + 8 kept within 0 .. 127; entries of one row block may repeat.
All inputs are finite; a program needn't handle non-finite values.
Results may differ from the reference program's by a relative error of at most 0.0043.
Values may be sent and summed in bfloat16 or wider, within the bound.
A program may use at most 64 MiB of HBM per device.

```python
import jax
import jax.numpy as jnp
from jax import lax

M = 16384
BLK = 128
NBLK = 6
SHOTS = 56
TICKS = 8
LAYERS = 32
RB = 128
RBD = 8


def draw_col_blocks(key, part):
    row_ids = jnp.arange(RB, dtype=jnp.int32)[None, :, None]
    slot_ids = jnp.arange(NBLK, dtype=jnp.int32)[None, None, :]
    offsets = jax.random.randint(key, (LAYERS, RB, NBLK), -RBD, RBD + 1, dtype=jnp.int32)
    offsets = jnp.where(slot_ids == 0, 0, jnp.where(slot_ids == 1, -RBD, jnp.where(slot_ids == 2, RBD, offsets)))
    return jnp.clip(row_ids + offsets, 0, RB - 1).astype(jnp.int32)


def levels(rng, extent, shards, smallest, largest):
    gain = 1.0
    for dim, blocks in shards:
        steps = jax.random.uniform(jax.random.fold_in(jax.random.fold_in(rng, 6), dim), (blocks,), jnp.float32, smallest / len(shards), largest / len(shards))
        gain = gain * jnp.repeat(jnp.exp(steps), extent[dim] // blocks).reshape((-1,) + (1,) * (len(extent) - 1 - dim))
    return gain


def centred(own_key, extent, scale, bound, cuts=(), held_as=jnp.bfloat16):
    factor_of = levels(own_key, extent, cuts, -0.22, 0.18) if cuts else 1.0
    values = jax.random.normal(own_key, extent, jnp.float32) * scale * factor_of
    return jnp.minimum(jnp.maximum(values, -bound), bound).astype(held_as)


def setup_inputs(seed: int = 0) -> dict:
    splits = jax.random.split(jax.random.key(seed), 5)
    propagator = centred(splits[0], (LAYERS, M, NBLK, BLK), (2 * NBLK * BLK) ** -0.5, 0.15625, ((0, 32), (1, 16)), jnp.float32)
    col_blocks = draw_col_blocks(jax.random.fold_in(splits[4], 71), 0)
    sources = centred(splits[2], (TICKS, LAYERS, SHOTS, M), 1.0, 6.0, ((1, 32), (3, 16)))
    incoming = centred(splits[3], (LAYERS, SHOTS, M), 1.0, 6.0, ((0, 32), (2, 16)))
    return dict(propagator=propagator, col_blocks=col_blocks, sources=sources, incoming=incoming)


def apply_layer(layer_prop, layer_cols, arriving, layer_source):
    shot_count = arriving.shape[0]
    blocks = arriving.astype(jnp.float32).reshape(shot_count, RB, BLK)
    picked = blocks[:, layer_cols, :]
    weights = layer_prop.reshape(RB, BLK, NBLK, BLK)
    mixed_rows = jnp.einsum('srkc,rbkc->srb', picked, weights, precision=lax.Precision.HIGHEST)
    total = mixed_rows.reshape(shot_count, M) + layer_source.astype(jnp.float32)
    return total.astype(jnp.bfloat16)


def reference(propagator, col_blocks, sources, incoming):
    arriving = incoming
    history = []
    for tick_index in range(TICKS):
        produced = lax.map(lambda packed: apply_layer(packed[0], packed[1], packed[2], packed[3]),
                           (propagator, col_blocks, arriving, sources[tick_index]))
        history.append(produced)
        arriving = jnp.concatenate([jnp.zeros_like(produced[:1]), produced[:-1]], axis=0)
    return jnp.stack(history)
```

```python
import jax
import jax.numpy as jnp
from jax import lax
from jax.experimental import pallas as pl
from jax.experimental.pallas import tpu as pltpu
from jax.sharding import PartitionSpec as P

BLK = 128
NBLK = 6
TICKS = 8
SLOTS = 4
CHUNKS = ((0, 16), (16, 16), (32, 16), (48, 8))
MESH = pl.DeviceIdType.MESH


def kernel(
    prop_hbm, cols_hbm, src_hbm, inc_hbm, out_hbm,
    prop, weights, cols, src, win, cur, obuf,
    prop_sem, cols_sem, src_sem, inc_sem, out_sem, send_sem, recv_sem, halo_send, halo_recv,
):
    layers = lax.axis_size("layer")
    places = lax.axis_size("row")
    layer = lax.axis_index("layer")
    place = lax.axis_index("row")
    width = obuf.shape[2]
    row_blocks = width // BLK
    has_left = place > 0
    has_right = place < places - 1
    has_next = layer < layers - 1
    has_prev = layer > 0

    inc_copy = pltpu.make_async_copy(inc_hbm.at[0], win.at[0, place % SLOTS], inc_sem)
    inc_copy.start()
    cols_copy = pltpu.make_async_copy(cols_hbm, cols, cols_sem)
    cols_copy.start()
    prop_copies = []
    for j in range(row_blocks):
        rows = pl.ds(j * BLK, BLK)
        prop_copies.append(
            pltpu.make_async_copy(prop_hbm.at[:, rows, :], prop.at[:, rows, :], prop_sem.at[j])
        )
        prop_copies[-1].start()
    src_copy = pltpu.make_async_copy(src_hbm.at[:, 0], src, src_sem)
    src_copy.start()

    barrier = pltpu.get_barrier_semaphore()

    def greet(ok, to_layer, to_place):
        @pl.when(ok)
        def _():
            pl.semaphore_signal(
                barrier, inc=1, device_id={"layer": to_layer, "row": to_place}, device_id_type=MESH
            )

    greet(has_left, layer, place - 1)
    greet(has_right, layer, place + 1)
    greet(has_prev, layer - 1, place)
    greet(jnp.logical_and(has_prev, has_left), layer - 1, place - 1)
    greet(jnp.logical_and(has_prev, has_right), layer - 1, place + 1)
    left_n = has_left.astype(jnp.int32)
    right_n = has_right.astype(jnp.int32)
    next_n = has_next.astype(jnp.int32)
    pl.semaphore_wait(barrier, left_n + right_n + next_n * (1 + left_n + right_n))

    inc_copy.wait()

    sides = ((has_left, -1), (has_right, 1))
    slot = place % SLOTS

    def halo(c, side):
        start, size = CHUNKS[c]
        ok, step = sides[side]
        rows = pl.ds(start, size)
        return ok, pltpu.make_async_remote_copy(
            src_ref=win.at[0, slot, rows, :],
            dst_ref=win.at[0, slot, rows, :],
            send_sem=halo_send.at[c, side],
            recv_sem=halo_recv.at[c, side],
            device_id={"layer": layer, "row": place + step},
            device_id_type=MESH,
        )

    for c in range(len(CHUNKS)):
        for side in range(2):
            ok, copy = halo(c, side)
            pl.when(ok)(copy.start)

    for j in range(row_blocks):
        prop_copies[j].wait()
        for k in range(NBLK):
            value = prop[k, j * BLK : (j + 1) * BLK, :]
            high = value.astype(jnp.bfloat16)
            low = (value - high.astype(jnp.float32)).astype(jnp.bfloat16)
            weights[j, 0:BLK, k * BLK : (k + 1) * BLK] = high
            weights[j, BLK : 2 * BLK, k * BLK : (k + 1) * BLK] = low

    @pl.when(layer == 0)
    def _():
        win[1:] = jnp.zeros((TICKS - 1,) + win.shape[1:], win.dtype)

    cols_copy.wait()
    picks = [[lax.rem(cols[k, 0, j], SLOTS * row_blocks) for k in range(NBLK)] for j in range(row_blocks)]
    src_copy.wait()

    targets = (
        (has_next, 0),
        (jnp.logical_and(has_next, has_left), -1),
        (jnp.logical_and(has_next, has_right), 1),
    )

    def forward(tick, c, which):
        start, size = CHUNKS[c]
        ok, step = targets[which]
        rows = pl.ds(start, size)
        return ok, pltpu.make_async_remote_copy(
            src_ref=obuf.at[tick, rows, :],
            dst_ref=win.at[(tick + 1) % TICKS, slot, rows, :],
            send_sem=send_sem.at[tick, c, which],
            recv_sem=recv_sem.at[tick, c, which],
            device_id={"layer": layer + 1, "row": place + step},
            device_id_type=MESH,
        )

    def store_out(tick, c):
        start, size = CHUNKS[c]
        rows = pl.ds(start, size)
        return pltpu.make_async_copy(obuf.at[tick, rows, :], out_hbm.at[tick, 0, rows, :], out_sem.at[tick, c])

    def compute(tick, c):
        start, size = CHUNKS[c]
        for step in (-1, 0, 1):
            near = (place + step + SLOTS) % SLOTS
            for b in range(row_blocks):
                cur[near * row_blocks + b, 0:size, :] = win[tick, near, start : start + size, b * BLK : (b + 1) * BLK]
        for j in range(row_blocks):
            picked = jnp.concatenate([cur[picks[j][k], 0:size, :] for k in range(NBLK)], axis=1)
            mixed = lax.dot_general(
                picked, weights[j], (((1,), (1,)), ((), ())), preferred_element_type=jnp.float32
            )
            total = mixed[:, 0:BLK] + mixed[:, BLK : 2 * BLK]
            added = src[tick, start : start + size, j * BLK : (j + 1) * BLK].astype(jnp.float32)
            obuf[tick, start : start + size, j * BLK : (j + 1) * BLK] = (total + added).astype(jnp.bfloat16)
        store_out(tick, c).start()

    for c in range(len(CHUNKS)):
        for side in range(2):
            ok = (has_right, has_left)[side]
            pl.when(ok)(halo(c, side)[1].wait_recv)
        compute(0, c)
        for which in range(3):
            ok, copy = forward(0, c, which)
            pl.when(ok)(copy.start)

    arrives = (
        has_prev,
        jnp.logical_and(has_prev, has_right),
        jnp.logical_and(has_prev, has_left),
    )

    @pl.loop(1, TICKS)
    def _(tick):
        for c in range(len(CHUNKS)):
            for which in range(3):
                pl.when(arrives[which])(forward(tick - 1, c, which)[1].wait_recv)
            compute(tick, c)
            for which in range(3):
                ok, copy = forward(tick, c, which)
                pl.when(jnp.logical_and(ok, tick < TICKS - 1))(copy.start)

    for c in range(len(CHUNKS)):
        for side in range(2):
            ok, copy = halo(c, side)
            pl.when(ok)(copy.wait_send)

    @pl.loop(0, TICKS)
    def _(tick):
        for c in range(len(CHUNKS)):
            for which in range(3):
                ok, copy = forward(tick, c, which)
                pl.when(jnp.logical_and(ok, tick < TICKS - 1))(copy.wait_send)
            store_out(tick, c).wait()


def body(propagator, col_blocks, sources, incoming):
    rows = propagator.shape[1]
    shots = incoming.shape[1]
    prop = jnp.transpose(propagator[0], (1, 0, 2))
    cols = jnp.transpose(col_blocks, (2, 0, 1))
    chunks = len(CHUNKS)
    return pl.pallas_call(
        kernel,
        name="sweep",
        out_shape=jax.ShapeDtypeStruct(sources.shape, jnp.bfloat16),
        in_specs=[pl.BlockSpec(memory_space=pl.ANY)] * 4,
        out_specs=pl.BlockSpec(memory_space=pl.ANY),
        scratch_shapes=[
            pltpu.VMEM((NBLK, rows, BLK), jnp.float32),
            pltpu.VMEM((rows // BLK, 2 * BLK, NBLK * BLK), jnp.bfloat16),
            pltpu.SMEM(cols.shape, jnp.int32),
            pltpu.VMEM((TICKS, shots, rows), jnp.bfloat16),
            pltpu.VMEM((TICKS, SLOTS, shots, rows), jnp.bfloat16),
            pltpu.VMEM((SLOTS * rows // BLK, 16, BLK), jnp.bfloat16),
            pltpu.VMEM((TICKS, shots, rows), jnp.bfloat16),
            pltpu.SemaphoreType.DMA((rows // BLK,)),
            pltpu.SemaphoreType.DMA,
            pltpu.SemaphoreType.DMA,
            pltpu.SemaphoreType.DMA,
            pltpu.SemaphoreType.DMA((TICKS, chunks)),
            pltpu.SemaphoreType.DMA((TICKS, chunks, 3)),
            pltpu.SemaphoreType.DMA((TICKS, chunks, 3)),
            pltpu.SemaphoreType.DMA((chunks, 2)),
            pltpu.SemaphoreType.DMA((chunks, 2)),
        ],
        compiler_params=pltpu.CompilerParams(collective_id=0, has_side_effects=True),
    )(prop, cols, sources, incoming)


def solution(mesh):
    return jax.shard_map(
        body,
        mesh=mesh,
        in_specs=(
            P("layer", "row", None, None),
            P("layer", "row", None),
            P(None, "layer", None, "row"),
            P("layer", None, "row"),
        ),
        out_specs=P(None, "layer", None, "row"),
        check_vma=False,
    )
```

```python
import jax
import jax.numpy as jnp
from jax import lax
from jax.experimental import pallas as pl
from jax.experimental.pallas import tpu as pltpu
from jax.sharding import PartitionSpec as P

BLK = 128
NBLK = 6
TICKS = 8
SLOTS = 4
GROUP = 8
MESH = pl.DeviceIdType.MESH


def kernel(
    prop_hbm, cols_hbm, src_hbm, inc_hbm, out_hbm,
    prop, weights, cols, src, win, cur, obuf,
    prop_sem, cols_sem, src_sem, inc_sem, out_sem, send_sem, recv_sem, halo_send,
):
    layers = lax.axis_size("layer")
    places = lax.axis_size("row")
    layer = lax.axis_index("layer")
    place = lax.axis_index("row")
    steps, group, width = obuf.shape
    chunks = steps // TICKS
    row_blocks = width // BLK
    slot = place % SLOTS
    has_left = place > 0
    has_right = place < places - 1
    has_next = layer < layers - 1
    has_prev = layer > 0

    inc_copy = pltpu.make_async_copy(inc_hbm, win.at[pl.ds(0, chunks), slot], inc_sem)
    inc_copy.start()
    cols_copy = pltpu.make_async_copy(cols_hbm, cols, cols_sem)
    cols_copy.start()
    prop_copies = []
    for j in range(row_blocks):
        rows = pl.ds(j * BLK, BLK)
        prop_copies.append(
            pltpu.make_async_copy(prop_hbm.at[:, rows, :], prop.at[:, rows, :], prop_sem.at[j])
        )
        prop_copies[-1].start()
    src_copy = pltpu.make_async_copy(src_hbm, src, src_sem)
    src_copy.start()

    barrier = pltpu.get_barrier_semaphore()

    def greet(ok, to_layer, to_place):
        @pl.when(ok)
        def _():
            pl.semaphore_signal(
                barrier, inc=1, device_id={"layer": to_layer, "row": to_place}, device_id_type=MESH
            )

    greet(has_prev & has_left, layer - 1, place - 1)
    greet(has_prev & has_right, layer - 1, place + 1)
    greet(has_left, layer, place - 1)
    greet(has_right, layer, place + 1)
    greet(has_prev, layer - 1, place)

    for j in range(row_blocks):
        prop_copies[j].wait()
        for k in range(NBLK):
            value = prop[k, j * BLK : (j + 1) * BLK, :].T
            high = value.astype(jnp.bfloat16)
            low = (value - high.astype(jnp.float32)).astype(jnp.bfloat16)
            weights[j, k * BLK : (k + 1) * BLK, 0:BLK] = high
            weights[j, k * BLK : (k + 1) * BLK, BLK : 2 * BLK] = low

    left_n = has_left.astype(jnp.int32)
    right_n = has_right.astype(jnp.int32)
    next_n = has_next.astype(jnp.int32)
    pl.semaphore_wait(barrier, left_n + right_n + next_n * (1 + left_n + right_n))

    inc_copy.wait()

    def halo(c, side):
        return pltpu.make_async_remote_copy(
            src_ref=win.at[c, slot],
            dst_ref=win.at[c, slot],
            send_sem=halo_send.at[c, side],
            recv_sem=recv_sem.at[c, side],
            device_id={"layer": layer, "row": place + (-1, 1)[side]},
            device_id_type=MESH,
        )

    for c in range(chunks):
        pl.when(has_left)(halo(c, 0).start)
        pl.when(has_right)(halo(c, 1).start)

    @pl.when(layer == 0)
    def _():
        win[chunks:] = jnp.zeros((steps - chunks,) + win.shape[1:], win.dtype)

    cols_copy.wait()
    picks = [[lax.rem(cols[k, 0, j], SLOTS * row_blocks) for k in range(NBLK)] for j in range(row_blocks)]
    src_copy.wait()

    def forward(step, which):
        return pltpu.make_async_remote_copy(
            src_ref=obuf.at[step],
            dst_ref=win.at[(step + chunks) % steps, slot],
            send_sem=send_sem.at[step, which],
            recv_sem=recv_sem.at[(step + chunks) % steps, which],
            device_id={"layer": layer + 1, "row": place + (-1, 1, 0)[which]},
            device_id_type=MESH,
        )

    def arrival(step, which):
        return pltpu.make_async_remote_copy(
            src_ref=win.at[step, slot],
            dst_ref=win.at[step, slot],
            send_sem=send_sem.at[step, which],
            recv_sem=recv_sem.at[step, which],
            device_id={"layer": layer, "row": place},
            device_id_type=MESH,
        )

    def store_out(step):
        return pltpu.make_async_copy(obuf.at[step], out_hbm.at[step], out_sem.at[step])

    sends = ((0, has_next & has_left), (1, has_next & has_right), (2, has_next))

    @pl.loop(0, steps)
    def _(step):
        first = step < chunks
        pl.when((first | has_prev) & has_right)(arrival(step, 0).wait_recv)
        pl.when((first | has_prev) & has_left)(arrival(step, 1).wait_recv)
        pl.when(jnp.logical_not(first) & has_prev)(arrival(step, 2).wait_recv)
        for shift in (-1, 0, 1):
            near = (place + shift + SLOTS) % SLOTS
            for b in range(row_blocks):
                cur[near * row_blocks + b] = win[step, near, :, b * BLK : (b + 1) * BLK]
        for j in range(row_blocks):
            picked = jnp.concatenate([cur[picks[j][k]] for k in range(NBLK)], axis=1)
            mixed = lax.dot_general(
                picked, weights[j], (((1,), (0,)), ((), ())), preferred_element_type=jnp.float32
            )
            total = mixed[:, 0:BLK] + mixed[:, BLK : 2 * BLK]
            added = src[step, :, j * BLK : (j + 1) * BLK].astype(jnp.float32)
            obuf[step, :, j * BLK : (j + 1) * BLK] = (total + added).astype(jnp.bfloat16)
        more = step < steps - chunks
        for which, ok in sends:
            pl.when(ok & more)(forward(step, which).start)
        store_out(step).start()

    for c in range(chunks):
        pl.when(has_left)(halo(c, 0).wait_send)
        pl.when(has_right)(halo(c, 1).wait_send)

    @pl.loop(0, steps)
    def _(step):
        more = step < steps - chunks
        for which, ok in sends:
            pl.when(ok & more)(forward(step, which).wait_send)
        store_out(step).wait()


def body(propagator, col_blocks, sources, incoming):
    rows = propagator.shape[1]
    ticks, _, shots, _ = sources.shape
    chunks = shots // GROUP
    steps = ticks * chunks
    prop = jnp.transpose(propagator[0], (1, 0, 2))
    cols = jnp.transpose(col_blocks, (2, 0, 1))
    out = pl.pallas_call(
        kernel,
        name="sweep",
        out_shape=jax.ShapeDtypeStruct((steps, GROUP, rows), jnp.bfloat16),
        in_specs=[pl.BlockSpec(memory_space=pl.ANY)] * 4,
        out_specs=pl.BlockSpec(memory_space=pl.ANY),
        scratch_shapes=[
            pltpu.VMEM((NBLK, rows, BLK), jnp.float32),
            pltpu.VMEM((rows // BLK, NBLK * BLK, 2 * BLK), jnp.bfloat16),
            pltpu.SMEM(cols.shape, jnp.int32),
            pltpu.VMEM((steps, GROUP, rows), jnp.bfloat16),
            pltpu.VMEM((steps, SLOTS, GROUP, rows), jnp.bfloat16),
            pltpu.VMEM((SLOTS * rows // BLK, GROUP, BLK), jnp.bfloat16),
            pltpu.VMEM((steps, GROUP, rows), jnp.bfloat16),
            pltpu.SemaphoreType.DMA((rows // BLK,)),
            pltpu.SemaphoreType.DMA,
            pltpu.SemaphoreType.DMA,
            pltpu.SemaphoreType.DMA,
            pltpu.SemaphoreType.DMA((steps,)),
            pltpu.SemaphoreType.DMA((steps, 3)),
            pltpu.SemaphoreType.DMA((steps, 3)),
            pltpu.SemaphoreType.DMA((chunks, 2)),
        ],
        compiler_params=pltpu.CompilerParams(collective_id=0, has_side_effects=True),
    )(
        prop,
        cols,
        sources.reshape(steps, GROUP, rows),
        incoming.reshape(chunks, GROUP, rows),
    )
    return out.reshape(sources.shape)


def solution(mesh):
    return jax.shard_map(
        body,
        mesh=mesh,
        in_specs=(
            P("layer", "row", None, None),
            P("layer", "row", None),
            P(None, "layer", None, "row"),
            P("layer", None, "row"),
        ),
        out_specs=P(None, "layer", None, "row"),
        check_vma=False,
    )
```

```python
import jax
import jax.numpy as jnp
from jax import lax
from jax.experimental import pallas as pl
from jax.experimental.pallas import tpu as pltpu
from jax.sharding import PartitionSpec as P

BLK = 128
NBLK = 6
TICKS = 8
SLOTS = 4
GROUP = 8
MESH = pl.DeviceIdType.MESH


def kernel(
    prop_hbm, cols_hbm, src_hbm, inc_hbm, obuf,
    prop, weights, cols, src, win, cur,
    prop_sem, cols_sem, src_sem, inc_sem, send_sem, recv_sem, halo_send,
):
    layers = lax.axis_size("layer")
    places = lax.axis_size("row")
    layer = lax.axis_index("layer")
    place = lax.axis_index("row")
    steps, group, width = obuf.shape
    chunks = steps // TICKS
    row_blocks = width // BLK
    slot = place % SLOTS
    has_left = place > 0
    has_right = place < places - 1
    inner = has_left & has_right
    has_next = layer < layers - 1
    has_prev = layer > 0

    inc_copy = pltpu.make_async_copy(inc_hbm, win.at[pl.ds(0, chunks), slot], inc_sem)
    inc_copy.start()
    cols_copy = pltpu.make_async_copy(cols_hbm, cols, cols_sem)
    cols_copy.start()
    prop_copies = []
    for j in range(row_blocks):
        rows = pl.ds(j * BLK, BLK)
        prop_copies.append(
            pltpu.make_async_copy(prop_hbm.at[:, rows, :], prop.at[:, rows, :], prop_sem.at[j])
        )
        prop_copies[-1].start()
    src_copy = pltpu.make_async_copy(src_hbm, src, src_sem)
    src_copy.start()

    barrier = pltpu.get_barrier_semaphore()

    def greet(ok, to_layer, to_place):
        @pl.when(ok)
        def _():
            pl.semaphore_signal(
                barrier, inc=1, device_id={"layer": to_layer, "row": to_place}, device_id_type=MESH
            )

    greet(has_prev & has_left, layer - 1, place - 1)
    greet(has_prev & has_right, layer - 1, place + 1)
    greet(has_left, layer, place - 1)
    greet(has_right, layer, place + 1)
    greet(has_prev, layer - 1, place)

    def prepare(blocks):
        for j in blocks:
            prop_copies[j].wait()
            for k in range(NBLK):
                value = prop[k, j * BLK : (j + 1) * BLK, :].T
                high = value.astype(jnp.bfloat16)
                low = (value - high.astype(jnp.float32)).astype(jnp.bfloat16)
                weights[j, k * BLK : (k + 1) * BLK, 0:BLK] = high
                weights[j, k * BLK : (k + 1) * BLK, BLK : 2 * BLK] = low

    prepare(range(0, row_blocks // 2))
    left_n = has_left.astype(jnp.int32)
    right_n = has_right.astype(jnp.int32)
    next_n = has_next.astype(jnp.int32)
    pl.semaphore_wait(barrier, left_n + right_n + next_n * (1 + left_n + right_n))

    inc_copy.wait()

    def halo(c, side):
        return pltpu.make_async_remote_copy(
            src_ref=win.at[c, slot],
            dst_ref=win.at[c, slot],
            send_sem=halo_send.at[side],
            recv_sem=recv_sem.at[c],
            device_id={"layer": layer, "row": place + (-1, 1)[side]},
            device_id_type=MESH,
        )

    for c in range(chunks):
        pl.when(has_left)(halo(c, 0).start)
        pl.when(has_right)(halo(c, 1).start)

    prepare(range(row_blocks // 2, row_blocks))

    @pl.when(layer == 0)
    def _():
        win[chunks:] = jnp.zeros((steps - chunks,) + win.shape[1:], win.dtype)

    cols_copy.wait()
    picks = [[lax.rem(cols[k, 0, j], SLOTS * row_blocks) for k in range(NBLK)] for j in range(row_blocks)]
    src_copy.wait()

    def forward(step, which):
        return pltpu.make_async_remote_copy(
            src_ref=obuf.at[step],
            dst_ref=win.at[(step + chunks) % steps, slot],
            send_sem=send_sem.at[which],
            recv_sem=recv_sem.at[(step + chunks) % steps],
            device_id={"layer": layer + 1, "row": place + (-1, 1, 0)[which]},
            device_id_type=MESH,
        )

    def take(step, pieces):
        pieces = win.at[step, pl.ds(0, pieces)]
        pltpu.make_async_copy(pieces, pieces, recv_sem.at[step]).wait()

    sends = ((0, has_next & has_left), (1, has_next & has_right), (2, has_next))

    @pl.loop(0, steps)
    def _(step):
        first = step < chunks
        later = jnp.logical_not(first) & has_prev
        pl.when(later & inner)(lambda: take(step, 3))
        pl.when((later & jnp.logical_not(inner)) | (first & inner))(lambda: take(step, 2))
        pl.when(first & jnp.logical_not(inner))(lambda: take(step, 1))
        for shift in (-1, 0, 1):
            near = (place + shift + SLOTS) % SLOTS
            for b in range(row_blocks):
                cur[near * row_blocks + b] = win[step, near, :, b * BLK : (b + 1) * BLK]
        for j in range(row_blocks):
            picked = jnp.concatenate([cur[picks[j][k]] for k in range(NBLK)], axis=1)
            mixed = lax.dot_general(
                picked, weights[j], (((1,), (0,)), ((), ())), preferred_element_type=jnp.float32
            )
            total = mixed[:, 0:BLK] + mixed[:, BLK : 2 * BLK]
            added = src[step, :, j * BLK : (j + 1) * BLK].astype(jnp.float32)
            obuf[step, :, j * BLK : (j + 1) * BLK] = (total + added).astype(jnp.bfloat16)
        more = step < steps - chunks
        for which, ok in sends:
            pl.when(ok & more)(forward(step, which).start)

    def drained(ref, sem):
        pltpu.make_async_copy(ref, ref, sem).wait()

    for side, ok in ((0, has_left), (1, has_right)):
        pl.when(ok)(lambda: drained(win.at[pl.ds(0, chunks), slot], halo_send.at[side]))
    for which, ok in sends:
        pl.when(ok)(lambda: drained(obuf.at[pl.ds(0, steps - chunks)], send_sem.at[which]))


def stay(x):
    return pltpu.with_memory_space_constraint(x, pltpu.MemorySpace.HBM)


def body(propagator, col_blocks, sources, incoming):
    rows = propagator.shape[1]
    ticks, _, shots, _ = sources.shape
    chunks = shots // GROUP
    steps = ticks * chunks
    prop = jnp.transpose(propagator[0], (1, 0, 2))
    cols = jnp.transpose(col_blocks, (2, 0, 1))
    out = pl.pallas_call(
        kernel,
        name="sweep",
        out_shape=jax.ShapeDtypeStruct((steps, GROUP, rows), jnp.bfloat16),
        in_specs=[pl.BlockSpec(memory_space=pl.ANY)] * 4,
        out_specs=pl.BlockSpec(memory_space=pltpu.VMEM),
        scratch_shapes=[
            pltpu.VMEM((NBLK, rows, BLK), jnp.float32),
            pltpu.VMEM((rows // BLK, NBLK * BLK, 2 * BLK), jnp.bfloat16),
            pltpu.SMEM(cols.shape, jnp.int32),
            pltpu.VMEM((steps, GROUP, rows), jnp.bfloat16),
            pltpu.VMEM((steps, SLOTS, GROUP, rows), jnp.bfloat16),
            pltpu.VMEM((SLOTS * rows // BLK, GROUP, BLK), jnp.bfloat16),
            pltpu.SemaphoreType.DMA((rows // BLK,)),
            pltpu.SemaphoreType.DMA,
            pltpu.SemaphoreType.DMA,
            pltpu.SemaphoreType.DMA,
            pltpu.SemaphoreType.DMA((3,)),
            pltpu.SemaphoreType.DMA((steps,)),
            pltpu.SemaphoreType.DMA((2,)),
        ],
        compiler_params=pltpu.CompilerParams(collective_id=0, has_side_effects=True, vmem_limit_bytes=14 << 20),
    )(
        stay(prop),
        stay(cols),
        stay(sources.reshape(steps, GROUP, rows)),
        stay(incoming.reshape(chunks, GROUP, rows)),
    )
    return out.reshape(sources.shape)


def solution(mesh):
    return jax.shard_map(
        body,
        mesh=mesh,
        in_specs=(
            P("layer", "row", None, None),
            P("layer", "row", None),
            P(None, "layer", None, "row"),
            P("layer", None, "row"),
        ),
        out_specs=P(None, "layer", None, "row"),
        check_vma=False,
    )
```

```python
import jax
import jax.numpy as jnp
from jax import lax
from jax.experimental import pallas as pl
from jax.experimental.pallas import tpu as pltpu
from jax.sharding import PartitionSpec as P

BLK = 128
NBLK = 6
TICKS = 8
SLOTS = 4
GROUP = 8
MESH = pl.DeviceIdType.MESH


def kernel(
    prop_hbm, cols_hbm, src_hbm, inc_hbm, obuf,
    prop, weights, cols, src, win, cur,
    prop_sem, cols_sem, src_sem, inc_sem, send_sem, recv_sem, halo_send,
):
    layers = lax.axis_size("layer")
    places = lax.axis_size("row")
    layer = lax.axis_index("layer")
    place = lax.axis_index("row")
    steps, group, width = obuf.shape
    chunks = steps // TICKS
    row_blocks = width // BLK
    slot = place % SLOTS
    has_left = place > 0
    has_right = place < places - 1
    inner = has_left & has_right
    has_next = layer < layers - 1
    has_prev = layer > 0

    inc_copy = pltpu.make_async_copy(inc_hbm, win.at[pl.ds(0, chunks), slot], inc_sem)
    inc_copy.start()
    cols_copy = pltpu.make_async_copy(cols_hbm, cols, cols_sem)
    cols_copy.start()
    prop_copies = []
    for j in range(row_blocks):
        rows = pl.ds(j * BLK, BLK)
        prop_copies.append(
            pltpu.make_async_copy(prop_hbm.at[:, rows, :], prop.at[:, rows, :], prop_sem.at[j])
        )
        prop_copies[-1].start()
    src_copy = pltpu.make_async_copy(src_hbm, src, src_sem)
    src_copy.start()

    barrier = pltpu.get_barrier_semaphore()

    def greet(ok, to_layer, to_place):
        @pl.when(ok)
        def _():
            pl.semaphore_signal(
                barrier, inc=1, device_id={"layer": to_layer, "row": to_place}, device_id_type=MESH
            )

    greet(has_left, layer, place - 1)
    greet(has_right, layer, place + 1)
    greet(has_prev, layer - 1, place)

    def prepare(blocks):
        for j in blocks:
            prop_copies[j].wait()
            for k in range(NBLK):
                value = prop[k, j * BLK : (j + 1) * BLK, :].T
                weights[j, k * BLK : (k + 1) * BLK, :] = value.astype(jnp.bfloat16)

    left_n = has_left.astype(jnp.int32)
    right_n = has_right.astype(jnp.int32)
    next_n = has_next.astype(jnp.int32)
    pl.semaphore_wait(barrier, left_n + right_n + next_n)

    inc_copy.wait()

    def halo(c, side):
        return pltpu.make_async_remote_copy(
            src_ref=win.at[c, slot],
            dst_ref=win.at[c, slot],
            send_sem=halo_send.at[side],
            recv_sem=recv_sem.at[c],
            device_id={"layer": layer, "row": place + (-1, 1)[side]},
            device_id_type=MESH,
        )

    for c in range(chunks):
        pl.when(has_left)(halo(c, 0).start)
        pl.when(has_right)(halo(c, 1).start)

    prepare(range(row_blocks))

    @pl.when(layer == 0)
    def _():
        win[chunks:] = jnp.zeros((steps - chunks,) + win.shape[1:], win.dtype)

    cols_copy.wait()
    picks = [[lax.rem(cols[k, 0, j], SLOTS * row_blocks) for k in range(NBLK)] for j in range(row_blocks)]
    src_copy.wait()

    def forward(step, which):
        return pltpu.make_async_remote_copy(
            src_ref=obuf.at[step],
            dst_ref=win.at[(step + chunks) % steps, slot],
            send_sem=send_sem.at[which],
            recv_sem=recv_sem.at[(step + chunks) % steps],
            device_id={"layer": layer + 1, "row": place + (-1, 1, 0)[which]},
            device_id_type=MESH,
        )

    def take(step, pieces):
        pieces = win.at[step, pl.ds(0, pieces)]
        pltpu.make_async_copy(pieces, pieces, recv_sem.at[step]).wait()

    sends = ((0, has_next & has_left), (1, has_next & has_right), (2, has_next))

    @pl.loop(0, steps)
    def _(step):
        first = step < chunks
        later = jnp.logical_not(first) & has_prev
        pl.when(later & inner)(lambda: take(step, 3))
        pl.when((later & jnp.logical_not(inner)) | (first & inner))(lambda: take(step, 2))
        pl.when(first & jnp.logical_not(inner))(lambda: take(step, 1))
        for shift in (-1, 0, 1):
            near = (place + shift + SLOTS) % SLOTS
            for b in range(row_blocks):
                cur[near * row_blocks + b] = win[step, near, :, b * BLK : (b + 1) * BLK]
        for j in range(row_blocks):
            picked = jnp.concatenate([cur[picks[j][k]] for k in range(NBLK)], axis=1)
            mixed = lax.dot_general(
                picked, weights[j], (((1,), (0,)), ((), ())), preferred_element_type=jnp.float32
            )
            total = mixed
            added = src[step, :, j * BLK : (j + 1) * BLK].astype(jnp.float32)
            obuf[step, :, j * BLK : (j + 1) * BLK] = (total + added).astype(jnp.bfloat16)
        more = step < steps - chunks
        for which, ok in sends:
            pl.when(ok & more)(forward(step, which).start)

    def drained(ref, sem):
        pltpu.make_async_copy(ref, ref, sem).wait()

    for side, ok in ((0, has_left), (1, has_right)):
        pl.when(ok)(lambda: drained(win.at[pl.ds(0, chunks), slot], halo_send.at[side]))
    for which, ok in sends:
        pl.when(ok)(lambda: drained(obuf.at[pl.ds(0, steps - chunks)], send_sem.at[which]))


def stay(x):
    return pltpu.with_memory_space_constraint(x, pltpu.MemorySpace.HBM)


def body(propagator, col_blocks, sources, incoming):
    rows = propagator.shape[1]
    ticks, _, shots, _ = sources.shape
    chunks = shots // GROUP
    steps = ticks * chunks
    prop = jnp.transpose(propagator[0], (1, 0, 2))
    cols = jnp.transpose(col_blocks, (2, 0, 1))
    out = pl.pallas_call(
        kernel,
        name="sweep",
        out_shape=jax.ShapeDtypeStruct((steps, GROUP, rows), jnp.bfloat16),
        in_specs=[pl.BlockSpec(memory_space=pl.ANY)] * 4,
        out_specs=pl.BlockSpec(memory_space=pltpu.VMEM),
        scratch_shapes=[
            pltpu.VMEM((NBLK, rows, BLK), jnp.float32),
            pltpu.VMEM((rows // BLK, NBLK * BLK, BLK), jnp.bfloat16),
            pltpu.SMEM(cols.shape, jnp.int32),
            pltpu.VMEM((steps, GROUP, rows), jnp.bfloat16),
            pltpu.VMEM((steps, SLOTS, GROUP, rows), jnp.bfloat16),
            pltpu.VMEM((SLOTS * rows // BLK, GROUP, BLK), jnp.bfloat16),
            pltpu.SemaphoreType.DMA((rows // BLK,)),
            pltpu.SemaphoreType.DMA,
            pltpu.SemaphoreType.DMA,
            pltpu.SemaphoreType.DMA,
            pltpu.SemaphoreType.DMA((3,)),
            pltpu.SemaphoreType.DMA((steps,)),
            pltpu.SemaphoreType.DMA((2,)),
        ],
        compiler_params=pltpu.CompilerParams(collective_id=0, has_side_effects=True, vmem_limit_bytes=14 << 20),
    )(
        stay(prop),
        stay(cols),
        stay(sources.reshape(steps, GROUP, rows)),
        stay(incoming.reshape(chunks, GROUP, rows)),
    )
    return out.reshape(sources.shape)


def solution(mesh):
    return jax.shard_map(
        body,
        mesh=mesh,
        in_specs=(
            P("layer", "row", None, None),
            P("layer", "row", None),
            P(None, "layer", None, "row"),
            P("layer", None, "row"),
        ),
        out_specs=P(None, "layer", None, "row"),
        check_vma=False,
    )
```
